512 devices in a mesh: pair: 16 (over x, z_lo), side: 2 (over core), rows: 16 (over z_hi, y).
Axes of the slice: x: 4, y: 4, z: 16 (z_hi: 4, z_lo: 4; z = z_hi * 4 + z_lo), core: 2. Of those that a mesh axis runs over, the one named last changes fastest.
Arguments:
- face_out: float32 [16, 2048, 768], P('pair', ('side', 'rows')), as said below
- face_in: float32 [16, 768, 7680], P('pair', 'rows', 'side'), as said below
- face_shared: float32 [16, 2, 768, 768], P('pair', 'side', 'rows'), as said below
Outputs:
- correction_t: float32 [16, 2, 3840, 2048], P('pair', None, 'rows', 'side')
- mean_square: float32 [], replicated
Inputs may be any that keep to these rules, and one draw needn't show every extreme that they name: `face_out`: float entries of order one over the square root of 768 or less. `face_in`: float entries. `face_shared`: each block is symmetric and positive definite, so the sum of a pair's two blocks is too.
All inputs are finite; a program needn't handle non-finite values.
Results may differ from the reference program's by a relative error of at most 0.0003.
Values sent between devices are 32-bit elements; how exact they have to be, the bound alone decides.
A program may use at most 64 MiB of HBM per device.

```python
import jax
import jax.numpy as jnp
from jax import lax

SH = 768
OUTC = 3840
OUTR = 1024
NPAIR = 16


def draw_face_out(key, part):
    keys = jax.random.split(jax.random.fold_in(key, 11), 2)
    shape = (NPAIR, 2 * OUTR, SH)
    row_scale = jnp.exp(jax.random.uniform(keys[0], (NPAIR, 2 * OUTR, 1), jnp.float32, jnp.log(0.3), jnp.log(3.0)))
    steps = jnp.arange(NPAIR).astype(jnp.float32) / max(NPAIR - 1, 1)
    pair_scale = jnp.sqrt(3.0) ** steps
    base = jnp.clip(jax.random.normal(keys[1], shape, jnp.float32), -4.0, 4.0)
    return base * row_scale * pair_scale[:, None, None] / jnp.sqrt(float(SH))


def draw_face_in(key, part):
    keys = jax.random.split(jax.random.fold_in(key, 23), 2)
    shape = (NPAIR, SH, 2 * OUTC)
    col_scale = jnp.exp(jax.random.uniform(keys[0], (NPAIR, 1, 2 * OUTC), jnp.float32, jnp.log(0.3), jnp.log(3.0)))
    base = jnp.clip(jax.random.normal(keys[1], shape, jnp.float32), -4.0, 4.0)
    return 0.025 * base * col_scale


def draw_face_shared(key, part):
    keys = jax.random.split(jax.random.fold_in(key, 37), 3)
    basis = jnp.clip(jax.random.normal(keys[0], (NPAIR, SH, SH), jnp.float32), -4.0, 4.0)
    ortho, upper = jnp.linalg.qr(basis)
    level = jnp.exp(jax.random.uniform(keys[1], (NPAIR, 1, SH), jnp.float32, jnp.log(0.01), jnp.log(2.0)))
    share = jnp.exp(jax.random.uniform(keys[2], (NPAIR, 2, SH), jnp.float32, jnp.log(0.5), jnp.log(2.0)))
    values = level * share
    scaled = ortho[:, None, :, :] * values[:, :, None, :]
    blocks = jnp.einsum('psik,pjk->psij', scaled, ortho, precision=lax.Precision.HIGHEST)
    return 0.5 * (blocks + jnp.swapaxes(blocks, 2, 3))


def setup_inputs(seed: int = 0) -> dict:
    arg_keys = jax.random.split(jax.random.key(seed), 4)
    face_out = draw_face_out(jax.random.fold_in(arg_keys[3], 71), 0)
    face_in = draw_face_in(jax.random.fold_in(arg_keys[3], 71), 0)
    face_shared = draw_face_shared(jax.random.fold_in(arg_keys[3], 71), 0)
    return {"face_out": face_out, "face_in": face_in, "face_shared": face_shared}


def merge_pair(operands):
    out_rows, in_cols, shared = operands
    schur = shared[0] + shared[1]
    factor = jnp.linalg.cholesky(schur)
    solved = jax.scipy.linalg.cho_solve((factor, True), in_cols)
    product = jnp.dot(out_rows.astype(jnp.float32), solved.astype(jnp.float32), precision=lax.Precision.HIGHEST, preferred_element_type=jnp.float32)
    return jnp.reshape(-jnp.transpose(product), (2, OUTC, 2 * OUTR))

def reference(face_out, face_in, face_shared):
    correction_t = lax.map(merge_pair, (face_out, face_in, face_shared))
    mean_square = jnp.sum(correction_t * correction_t) / correction_t.size
    return (correction_t, mean_square)
```

```python
import jax
import jax.numpy as jnp
from jax import lax
from jax.experimental import pallas as pl
from jax.experimental.pallas import tpu as pltpu
from jax.sharding import PartitionSpec as P

MESH = pl.DeviceIdType.MESH
F32 = jnp.float32
BF16 = jnp.bfloat16
NB = 128
G = 8
Y = 4
ZH = 4
ROWS = Y * ZH
STEPS = ((0, 1), (0, 3), (0, 2), (1, 0), (3, 0), (1, 1), (1, 3), (3, 1), (3, 3), (1, 2), (3, 2), (2, 0), (2, 1), (2, 3), (2, 2))


def sweep_tile(tile):
    row = lax.broadcasted_iota(jnp.int32, (G, NB), 0)
    lane = lax.broadcasted_iota(jnp.int32, (G, NB), 1)
    wide = lax.broadcasted_iota(jnp.int32, (NB, NB), 1)
    for k in range(0, NB, G):
        cols = [jnp.broadcast_to(tile[:, k + u : k + u + 1], (NB, NB)) for u in range(G)]
        d = {(t, u): jnp.broadcast_to(cols[u][k + t : k + t + 1, :], (G, NB)) for u in range(G) for t in range(u + 1)}
        inside = (lane >= k) & (lane < k + G)
        pivots = jnp.where(inside, jnp.where(lane - k == row, -1.0, 0.0), tile[k : k + G, :])
        v = [jnp.broadcast_to(pivots[t : t + 1, :], (G, NB)) for t in range(G)]
        r, low = [None] * G, {}
        for t in range(G):
            r[t] = 1.0 / d[t, t]
            for u in range(t + 1, G):
                low[t, u] = d[t, u] * r[t]
            for u in range(t + 1, G):
                for x in range(u, G):
                    d[u, x] = d[u, x] - low[t, u] * d[t, x]
                v[u] = v[u] - low[t, u] * v[t]
        w = [v[t] * r[t] for t in range(G)]
        for t in range(G - 1, 0, -1):
            for u in range(t):
                w[u] = w[u] - low[u, t] * w[t]
        acc = jnp.where((wide >= k) & (wide < k + G), 0.0, tile)
        for t in range(G):
            acc = acc - cols[t] * jnp.broadcast_to(w[t][0:1, :], (NB, NB))
        packed = w[0]
        for t in range(1, G):
            packed = jnp.where(row == t, w[t], packed)
        tile = jnp.concatenate([x for x in (acc[:k], packed, acc[k + G :]) if x.shape[0]], axis=0)
    return tile


def split(x):
    hi = x.astype(BF16)
    return hi, (x - hi.astype(F32)).astype(BF16)


def dot3(a, b, dims):
    (ah, al), (bh, bl) = a, b
    one = lambda x, y: lax.dot_general(x, y, (dims, ((), ())), preferred_element_type=F32)
    return one(ah, bh) + (one(ah, bl) + one(al, bh))


def kernel(scale, panel_ref, in_ref, shared_ref, out_ref, mean_ref, schur, inv, rows_a, pieces, cols_b, xt_hi, xt_lo,
           half_in, acc, sum_r, sum_p, sum_s, half_s, half_r, sz_s, sz_r, sy_s, sy_r, sx_s, sx_r, az_s, az_r, ay_s, ay_r,
           b_s, b_r, bx_s, bx_r, pr_s, pr_r, pp_s, pp_r, ps_s, ps_r):
    me = lax.axis_index("rows")
    side = lax.axis_index("side")
    pair = lax.axis_index("pair")
    zh, y = me // Y, lax.rem(me, Y)
    n = 768
    half = 24
    width = 240
    pairs = 16

    def at(dz, dy):
        return lax.rem(zh + dz, ZH) * Y + lax.rem(y + dy, Y)

    def back(dz, dy):
        return lax.rem(zh + ZH - dz, ZH) * Y + lax.rem(y + Y - dy, Y)

    sibling = {"side": 1 - side}

    def remote(src, dst, send, recv, device):
        return pltpu.make_async_remote_copy(
            src_ref=src, dst_ref=dst, send_sem=send, recv_sem=recv, device_id=device, device_id_type=MESH
        )

    sends = []

    def send(src, dst, s, r, device):
        copy = remote(src, dst, s, r, device)
        copy.start()
        sends.append(copy)

    def arrived(dst, s, r):
        remote(dst, dst, s, r, sibling).wait_recv()

    barrier = pltpu.get_barrier_semaphore()
    pl.semaphore_signal(barrier, inc=1, device_id=sibling, device_id_type=MESH)
    for dz, dy in STEPS:
        pl.semaphore_signal(barrier, inc=1, device_id={"rows": at(dz, dy)}, device_id_type=MESH)
    for o in range(1, pairs):
        pl.semaphore_signal(barrier, inc=1, device_id={"pair": lax.rem(pair + o, pairs)}, device_id_type=MESH)
    pl.semaphore_wait(barrier, ROWS + pairs - 1)

    def strip(ref, r, s):
        return ref.at[pl.ds(pl.multiple_of((r * 2 + s) * half, 8), half), :]

    def panel_at(r):
        return rows_a.at[pl.ds(pl.multiple_of(r * 64, 64), 64), :]

    def columns_at(s, r):
        return cols_b.at[s, pl.ds(pl.multiple_of(r * 48, 16), 48), :]

    theirs = shared_ref.at[0, 0, pl.ds(pl.multiple_of((1 - side) * half, 8), half), :]
    send(theirs, half_in, half_s, half_r, sibling)
    arrived(half_in, half_s, half_r)
    mine = strip(schur, me, side)
    mine[...] = shared_ref[0, 0, pl.ds(pl.multiple_of(side * half, 8), half), :] + half_in[...]
    for i, dz in enumerate((1, 3, 2)):
        send(mine, mine, sz_s.at[i], sz_r.at[i], {"rows": at(dz, 0)})
    for i, dy in enumerate((1, 3, 2)):
        send(mine, mine, sy_s.at[0, i], sy_r.at[0, i], {"rows": at(0, dy)})
    send(mine, mine, sx_s.at[0], sx_r.at[0], sibling)

    panel = panel_ref.at[0]
    for i, dz in enumerate((1, 3, 2)):
        send(panel, panel_at(me), az_s.at[i], az_r.at[i], {"rows": at(dz, 0)})
    for r in range(ROWS):
        pieces[r, :, 0:width] = in_ref[0, :, r * width : (r + 1) * width]
        pieces[r, :, width:256] = jnp.zeros((48, 256 - width), F32)
    panel_at(me)[...] = panel_ref[0]
    columns_at(side, me)[...] = pieces[me]

    for i, dz in enumerate((1, 3, 2)):
        got = strip(schur, back(dz, 0), side)
        arrived(got, sz_s.at[i], sz_r.at[i])
        for j, dy in enumerate((1, 3, 2)):
            send(got, got, sy_s.at[i + 1, j], sy_r.at[i + 1, j], {"rows": at(0, dy)})
        send(got, got, sx_s.at[i + 1], sx_r.at[i + 1], sibling)
    for j, dy in enumerate((1, 3, 2)):
        send(panel, panel_at(me), ay_s.at[0, j], ay_r.at[0, j], {"rows": at(0, dy)})
    for i, (dz, dy) in enumerate(STEPS):
        send(pieces.at[at(dz, dy)], columns_at(side, me), b_s.at[i], b_r.at[i], {"rows": at(dz, dy)})
    for i, dz in enumerate((0, 1, 3, 2)):
        for j, dy in enumerate((1, 3, 2)):
            got = strip(schur, back(dz, dy), side)
            arrived(got, sy_s.at[i, j], sy_r.at[i, j])
            send(got, got, sx_s.at[4 + i * 3 + j], sx_r.at[4 + i * 3 + j], sibling)
    for i, dz in enumerate((0, 1, 3, 2)):
        arrived(strip(schur, back(dz, 0), 1 - side), sx_s.at[i], sx_r.at[i])
    for i, dz in enumerate((0, 1, 3, 2)):
        for j, dy in enumerate((1, 3, 2)):
            arrived(strip(schur, back(dz, dy), 1 - side), sx_s.at[4 + i * 3 + j], sx_r.at[4 + i * 3 + j])

    def onward_rows(i, dz):
        got = panel_at(back(dz, 0))
        return [
            remote(got, got, ay_s.at[i + 1, j], ay_r.at[i + 1, j], {"rows": at(0, dy)}) for j, dy in enumerate((1, 3, 2))
        ]

    def relay_rows(i, dz):
        arrived(panel_at(back(dz, 0)), az_s.at[i], az_r.at[i])
        for copy in onward_rows(i, dz):
            copy.start()

    def onward_columns(i, dz, dy):
        got = columns_at(side, back(dz, dy))
        return remote(got, got, bx_s.at[i], bx_r.at[i], sibling)

    def own_columns():
        got = columns_at(side, me)
        return remote(got, got, bx_s.at[15], bx_r.at[15], sibling)

    def relay_columns(i, dz, dy):
        arrived(columns_at(side, back(dz, dy)), b_s.at[i], b_r.at[i])
        onward_columns(i, dz, dy).start()

    inv[...] = schur[...]

    @pl.loop(0, n // NB)
    def _(b):
        @pl.when(b == 1)
        def _():
            relay_rows(0, 1)
            relay_rows(1, 3)

        @pl.when(b == 2)
        def _():
            relay_rows(2, 2)

        @pl.when(b == 3)
        def _():
            own_columns().start()
            for i in range(3):
                relay_columns(i, *STEPS[i])

        @pl.when(b == 5)
        def _():
            for i in range(3, 11):
                relay_columns(i, *STEPS[i])

        block = pl.ds(pl.multiple_of(b * NB, NB), NB)
        swept = sweep_tile(inv[block, block])
        eye = lax.broadcasted_iota(jnp.int32, (NB, NB), 0) == lax.broadcasted_iota(jnp.int32, (NB, NB), 1)
        column = inv[:, block]
        inv[block, block] = jnp.where(eye, -1.0, 0.0)
        w = jnp.dot(swept, inv[block, :], precision=lax.Precision.HIGHEST, preferred_element_type=F32)
        inv[:, block] = jnp.zeros((n, NB), F32)
        inv[...] = inv[...] + jnp.dot(column, w, precision=lax.Precision.HIGHEST, preferred_element_type=F32)
        inv[block, :] = -w

    for i in range(11, 15):
        relay_columns(i, *STEPS[i])
    arrived(columns_at(1 - side, me), bx_s.at[15], bx_r.at[15])
    for i, (dz, dy) in enumerate(STEPS):
        arrived(columns_at(1 - side, back(dz, dy)), bx_s.at[i], bx_r.at[i])
    for i, dz in enumerate((0, 1, 3, 2)):
        for j, dy in enumerate((1, 3, 2)):
            arrived(panel_at(back(dz, dy)), ay_s.at[i, j], ay_r.at[i, j])

    inverse = split(inv[...])
    for b in range(2):
        x = dot3(split(cols_b[b].T), inverse, ((1,), (0,)))
        xt_hi[b], xt_lo[b] = split(x)

    acc[...] = jnp.zeros((8, 128), F32)

    @pl.loop(0, 4)
    def _(i):
        tile = pl.ds(pl.multiple_of(i * 256, 256), 256)
        a = split(rows_a[tile, :])
        for b in range(2):
            c = dot3((xt_hi[b], xt_lo[b]), a, ((1,), (1,)))[:width]
            out_ref[0, b, :, tile] = c
            s = jnp.sum((c * c).reshape(width // 8, 8, 256), axis=0)
            acc[...] = acc[...] + (s[:, :128] + s[:, 128:])

    sum_r[me] = acc[...]
    for i, (dz, dy) in enumerate(STEPS):
        send(acc, sum_r.at[me], pr_s.at[i], pr_r.at[i], {"rows": at(dz, dy)})
    for i, (dz, dy) in enumerate(STEPS):
        arrived(sum_r.at[back(dz, dy)], pr_s.at[i], pr_r.at[i])
    sum_p[pair] = jnp.sum(sum_r[...], axis=0)
    for o in range(1, pairs):
        send(sum_p.at[pair], sum_p.at[pair], pp_s.at[o], pp_r.at[o], {"pair": lax.rem(pair + o, pairs)})
    for o in range(1, pairs):
        arrived(sum_p.at[lax.rem(pair + pairs - o, pairs)], pp_s.at[o], pp_r.at[o])
    total = jnp.sum(sum_p[...], axis=0)
    sum_s[side] = total
    send(sum_s.at[side], sum_s.at[side], ps_s, ps_r, sibling)
    arrived(sum_s.at[1 - side], ps_s, ps_r)
    mean_ref[0, 0] = jnp.sum(sum_s[0] + sum_s[1]) * scale
    for i, dz in enumerate((1, 3, 2)):
        sends.extend(onward_rows(i, dz))
    for i, (dz, dy) in enumerate(STEPS):
        sends.append(onward_columns(i, dz, dy))
    sends.append(own_columns())
    for copy in sends:
        copy.wait_send()


def body(face_out, face_in, face_shared):
    dma = pltpu.SemaphoreType.DMA
    vmem = pltpu.VMEM
    sems = [dma, dma, dma((3,)), dma((3,)), dma((4, 3)), dma((4, 3)), dma((16,)), dma((16,)), dma((3,)), dma((3,)), dma((4, 3)),
            dma((4, 3)), dma((15,)), dma((15,)), dma((16,)), dma((16,)), dma((15,)), dma((15,)), dma((16,)), dma((16,)), dma, dma]
    entries = 16 * 2 * 3840 * 2048
    out, mean = pl.pallas_call(
        lambda *refs: kernel(1.0 / entries, *refs),
        out_shape=(jax.ShapeDtypeStruct((1, 2, 240, 1024), F32), jax.ShapeDtypeStruct((1, 1), F32)),
        in_specs=[pl.BlockSpec(memory_space=vmem)] * 3,
        out_specs=(pl.BlockSpec(memory_space=vmem), pl.BlockSpec(memory_space=pltpu.SMEM)),
        scratch_shapes=[vmem((768, 768), F32), vmem((768, 768), F32), vmem((1024, 768), F32), vmem((16, 48, 256), F32),
                        vmem((2, 768, 256), F32), vmem((2, 256, 768), BF16), vmem((2, 256, 768), BF16), vmem((24, 768), F32),
                        vmem((8, 128), F32), vmem((16, 8, 128), F32), vmem((16, 8, 128), F32), vmem((2, 8, 128), F32)] + sems,
        compiler_params=pltpu.CompilerParams(collective_id=0, has_side_effects=True, vmem_limit_bytes=56 << 20),
        name="merge",
    )(face_out, face_in, face_shared)
    return out, mean[0, 0]


def solution(mesh):
    in_specs = (P("pair", ("side", "rows"), None), P("pair", "rows", "side"), P("pair", "side", "rows", None))
    out_specs = (P("pair", None, "rows", "side"), P())
    return jax.shard_map(body, mesh=mesh, in_specs=in_specs, out_specs=out_specs, check_vma=False)
```

```python
import jax
import jax.numpy as jnp
from jax import lax
from jax.experimental import pallas as pl
from jax.experimental.pallas import tpu as pltpu
from jax.sharding import PartitionSpec as P

MESH = pl.DeviceIdType.MESH
F32 = jnp.float32
BF16 = jnp.bfloat16
NB = 128
R = 32
G = 8
Y = 4
ZH = 4
ROWS = Y * ZH
STEPS = ((0, 1), (0, 3), (0, 2), (1, 0), (3, 0), (1, 1), (1, 3), (3, 1), (3, 3), (1, 2), (3, 2), (2, 0), (2, 1), (2, 3), (2, 2))


def sweep_tile(tile, one):
    row = lax.broadcasted_iota(jnp.int32, (G, NB), 0)
    lane = lax.broadcasted_iota(jnp.int32, (G, NB), 1)
    prow = lax.broadcasted_iota(jnp.int32, (R, NB), 0)
    plane = lax.broadcasted_iota(jnp.int32, (R, NB), 1)
    wide = lax.broadcasted_iota(jnp.int32, (NB, NB), 1)
    for p in range(0, NB, R):
        rows = tile[p : p + R, :]
        before = jnp.where((plane >= p) & (plane < p + R), jnp.where(plane - p == prow, -1.0, 0.0), rows)
        for g in range(0, R, G):
            k = p + g
            cols = [jnp.broadcast_to(rows[:, k + u : k + u + 1], (R, NB)) for u in range(G)]
            pivots = rows[g : g + G, :]
            inside = (lane >= k) & (lane < k + G)
            marked = jnp.where(inside, jnp.where(lane - k == row, -1.0, 0.0), pivots)
            v = [jnp.broadcast_to(marked[t : t + 1, :], (G, NB)) for t in range(G)]
            d = {}
            for t in range(G):
                full = jnp.broadcast_to(pivots[t : t + 1, :], (G, NB)) * one
                for u in range(t, G):
                    d[t, u] = jnp.broadcast_to(full[:, k + u : k + u + 1], (G, NB))
            r, low = [None] * G, {}
            for t in range(G):
                r[t] = 1.0 / d[t, t]
                for u in range(t + 1, G):
                    low[t, u] = d[t, u] * r[t]
                for u in range(t + 1, G):
                    for x in range(u, G):
                        d[u, x] = d[u, x] - low[t, u] * d[t, x]
                    v[u] = v[u] - low[t, u] * v[t]
            w = [v[t] * r[t] for t in range(G)]
            for t in range(G - 1, 0, -1):
                for u in range(t):
                    w[u] = w[u] - low[u, t] * w[t]
            packed = w[0]
            for t in range(1, G):
                packed = jnp.where(row == t, w[t], packed)
            acc = jnp.where((plane >= k) & (plane < k + G), 0.0, rows)
            for t in range(G):
                acc = acc - cols[t] * jnp.broadcast_to(w[t][0:1, :], (R, NB))
            rows = jnp.concatenate([x for x in (acc[:g], packed, acc[g + G :]) if x.shape[0]], axis=0)
        rest = jnp.where((wide >= p) & (wide < p + R), 0.0, tile)
        rest = rest - lax.dot_general(
            before, rows, (((0,), (0,)), ((), ())), precision=lax.Precision.HIGHEST, preferred_element_type=F32
        )
        tile = jnp.concatenate([x for x in (rest[:p], rows, rest[p + R :]) if x.shape[0]], axis=0)
    return tile


def split(x):
    hi = x.astype(BF16)
    return hi, (x - hi.astype(F32)).astype(BF16)


def dot3(a, b, dims):
    (ah, al), (bh, bl) = a, b
    one = lambda x, y: lax.dot_general(x, y, (dims, ((), ())), preferred_element_type=F32)
    return one(ah, bh) + (one(ah, bl) + one(al, bh))


def kernel(scale, panel_ref, in_ref, shared_ref, out_ref, mean_ref, schur, inv, rows_a, pieces, cols_b, xt_hi, xt_lo,
           half_in, product, one, acc, sum_r, sum_p, sum_s, half_s, half_r, sz_s, sz_r, sy_s, sy_r, sx_s, sx_r, az_s, az_r, ah_s, ah_r, ay_s, ay_r,
           b_s, b_r, bx_s, bx_r, pr_s, pr_r, pp_s, pp_r, ps_s, ps_r, o_s):
    me = lax.axis_index("rows")
    side = lax.axis_index("side")
    pair = lax.axis_index("pair")
    zh, y = me // Y, lax.rem(me, Y)
    n = 768
    half = 24
    width = 240
    pairs = 16

    def at(dz, dy):
        return lax.rem(zh + dz, ZH) * Y + lax.rem(y + dy, Y)

    def back(dz, dy):
        return lax.rem(zh + ZH - dz, ZH) * Y + lax.rem(y + Y - dy, Y)

    sibling = {"side": 1 - side}

    def remote(src, dst, send, recv, device):
        return pltpu.make_async_remote_copy(
            src_ref=src, dst_ref=dst, send_sem=send, recv_sem=recv, device_id=device, device_id_type=MESH
        )

    sends = []

    def send(src, dst, s, r, device):
        copy = remote(src, dst, s, r, device)
        copy.start()
        sends.append(copy)

    def arrived(dst, s, r):
        remote(dst, dst, s, r, sibling).wait_recv()

    barrier = pltpu.get_barrier_semaphore()
    pl.semaphore_signal(barrier, inc=1, device_id=sibling, device_id_type=MESH)
    for dz, dy in STEPS:
        pl.semaphore_signal(barrier, inc=1, device_id={"rows": at(dz, dy)}, device_id_type=MESH)
    for o in range(1, pairs):
        pl.semaphore_signal(barrier, inc=1, device_id={"pair": lax.rem(pair + o, pairs)}, device_id_type=MESH)

    def strip(ref, r, s):
        return ref.at[pl.ds(pl.multiple_of((r * 2 + s) * half, 8), half), :]

    def panel_at(r):
        return rows_a.at[pl.ds(pl.multiple_of(r * 64, 64), 64), :]

    def half_panel_at(r, h):
        return rows_a.at[pl.ds(pl.multiple_of(r * 64 + h * 32, 32), 32), :]

    def columns_at(s, r):
        return cols_b.at[s, pl.ds(pl.multiple_of(r * 48, 16), 48), :]

    for r in range(ROWS):
        pieces[r, :, 0:width] = in_ref[0, :, r * width : (r + 1) * width]
        pieces[r, :, width:256] = jnp.zeros((48, 256 - width), F32)
    panel_at(me)[...] = panel_ref[0]
    columns_at(side, me)[...] = pieces[me]
    one[...] = jnp.ones((G, NB), F32)
    pl.semaphore_wait(barrier, ROWS + pairs - 1)

    theirs = shared_ref.at[0, 0, pl.ds(pl.multiple_of((1 - side) * half, 8), half), :]
    send(theirs, half_in, half_s, half_r, sibling)
    arrived(half_in, half_s, half_r)
    mine = strip(schur, me, side)
    mine[...] = shared_ref[0, 0, pl.ds(pl.multiple_of(side * half, 8), half), :] + half_in[...]
    for i, dz in enumerate((1, 3, 2)):
        send(mine, mine, sz_s.at[i], sz_r.at[i], {"rows": at(dz, 0)})
    for i, dy in enumerate((1, 3, 2)):
        send(mine, mine, sy_s.at[0, i], sy_r.at[0, i], {"rows": at(0, dy)})
    send(mine, mine, sx_s.at[0], sx_r.at[0], sibling)

    panel = panel_ref.at[0]
    for i, dz in enumerate((1, 3)):
        send(panel, panel_at(me), az_s.at[i], az_r.at[i], {"rows": at(dz, 0)})

    for i, dz in enumerate((1, 3, 2)):
        got = strip(schur, back(dz, 0), side)
        arrived(got, sz_s.at[i], sz_r.at[i])
        for j, dy in enumerate((1, 3, 2)):
            send(got, got, sy_s.at[i + 1, j], sy_r.at[i + 1, j], {"rows": at(0, dy)})
        send(got, got, sx_s.at[i + 1], sx_r.at[i + 1], sibling)

    def columns_copy(i, dz, dy):
        return remote(pieces.at[at(dz, dy)], columns_at(side, me), b_s.at[i], b_r.at[i], {"rows": at(dz, dy)})

    for i in range(11):
        columns_copy(i, *STEPS[i]).start()
    for j, dy in enumerate((1, 3, 2)):
        send(panel, panel_at(me), ay_s.at[0, j], ay_r.at[0, j], {"rows": at(0, dy)})
    for i, dz in enumerate((0, 1, 3, 2)):
        for j, dy in enumerate((1, 3, 2)):
            got = strip(schur, back(dz, dy), side)
            arrived(got, sy_s.at[i, j], sy_r.at[i, j])
            send(got, got, sx_s.at[4 + i * 3 + j], sx_r.at[4 + i * 3 + j], sibling)
    for i, dz in enumerate((0, 1, 3, 2)):
        arrived(strip(schur, back(dz, 0), 1 - side), sx_s.at[i], sx_r.at[i])
    for i, dz in enumerate((0, 1, 3, 2)):
        for j, dy in enumerate((1, 3, 2)):
            arrived(strip(schur, back(dz, dy), 1 - side), sx_s.at[4 + i * 3 + j], sx_r.at[4 + i * 3 + j])

    def onward_rows(i, dz):
        got = panel_at(back(dz, 0))
        return [
            remote(got, got, ay_s.at[i + 1, j], ay_r.at[i + 1, j], {"rows": at(0, dy)}) for j, dy in enumerate((1, 3, 2))
        ]

    def start_rows(i, dz):
        for copy in onward_rows(i, dz):
            copy.start()

    def half_copies():
        first, last = half_panel_at(back(1, 0), 0), half_panel_at(back(3, 0), 1)
        return [
            remote(first, first, ah_s.at[0], ah_r.at[0], {"rows": at(1, 0)}),
            remote(last, last, ah_s.at[1], ah_r.at[1], {"rows": at(3, 0)}),
        ]

    def onward_columns(i, dz, dy):
        got = columns_at(side, back(dz, dy))
        return remote(got, got, bx_s.at[i], bx_r.at[i], sibling)

    def own_columns():
        got = columns_at(side, me)
        return remote(got, got, bx_s.at[15], bx_r.at[15], sibling)

    def relay_columns(i, dz, dy):
        arrived(columns_at(side, back(dz, dy)), b_s.at[i], b_r.at[i])
        onward_columns(i, dz, dy).start()

    inv[...] = schur[...]

    @pl.loop(0, n // NB)
    def _(b):
        @pl.when(b == 1)
        def _():
            for i, dz in enumerate((1, 3)):
                arrived(panel_at(back(dz, 0)), az_s.at[i], az_r.at[i])
            for copy in half_copies():
                copy.start()
            for i in range(11, 15):
                columns_copy(i, *STEPS[i]).start()
            start_rows(0, 1)
            start_rows(1, 3)

        @pl.when(b == 4)
        def _():
            own_columns().start()
            for i in range(11):
                relay_columns(i, *STEPS[i])

        @pl.when(b == 5)
        def _():
            for h in range(2):
                arrived(half_panel_at(back(2, 0), h), ah_s.at[h], ah_r.at[h])
            start_rows(2, 2)

        block = pl.ds(pl.multiple_of(b * NB, NB), NB)
        swept = sweep_tile(inv[block, block], one[...])
        eye = lax.broadcasted_iota(jnp.int32, (NB, NB), 0) == lax.broadcasted_iota(jnp.int32, (NB, NB), 1)
        column = inv[:, block]
        inv[block, block] = jnp.where(eye, -1.0, 0.0)
        w = jnp.dot(swept, inv[block, :], precision=lax.Precision.HIGHEST, preferred_element_type=F32)
        inv[:, block] = jnp.zeros((n, NB), F32)
        inv[...] = inv[...] + jnp.dot(column, w, precision=lax.Precision.HIGHEST, preferred_element_type=F32)
        inv[block, :] = -w

    inverse = split(inv[...])
    for i in range(11, 15):
        relay_columns(i, *STEPS[i])

    def solve(b):
        xt_hi[b], xt_lo[b] = split(dot3(split(cols_b[b].T), inverse, ((1,), (0,))))

    solve(side)
    arrived(columns_at(1 - side, me), bx_s.at[15], bx_r.at[15])
    for i, (dz, dy) in enumerate(STEPS):
        arrived(columns_at(1 - side, back(dz, dy)), bx_s.at[i], bx_r.at[i])
    solve(1 - side)
    for i, dz in enumerate((0, 1, 3, 2)):
        for j, dy in enumerate((1, 3, 2)):
            arrived(panel_at(back(dz, dy)), ay_s.at[i, j], ay_r.at[i, j])

    acc[...] = jnp.zeros((8, 128), F32)

    def out_copy(i, tile):
        return pltpu.make_async_copy(product.at[:, :, tile], out_ref.at[0, :, :, tile], o_s.at[i])

    @pl.loop(0, 4)
    def _(i):
        tile = pl.ds(pl.multiple_of(i * 256, 256), 256)
        a = split(rows_a[tile, :])
        for b in range(2):
            c = dot3((xt_hi[b], xt_lo[b]), a, ((1,), (1,)))[:width]
            product[b, :, tile] = c
            s = jnp.sum((c * c).reshape(width // 8, 8, 256), axis=0)
            acc[...] = acc[...] + (s[:, :128] + s[:, 128:])
        out_copy(i, tile).start()

    sum_r[me] = acc[...]
    for i, (dz, dy) in enumerate(STEPS):
        send(acc, sum_r.at[me], pr_s.at[i], pr_r.at[i], {"rows": at(dz, dy)})
    for i, (dz, dy) in enumerate(STEPS):
        arrived(sum_r.at[back(dz, dy)], pr_s.at[i], pr_r.at[i])
    sum_p[pair] = jnp.sum(sum_r[...], axis=0)
    for o in range(1, pairs):
        send(sum_p.at[pair], sum_p.at[pair], pp_s.at[o], pp_r.at[o], {"pair": lax.rem(pair + o, pairs)})
    for o in range(1, pairs):
        arrived(sum_p.at[lax.rem(pair + pairs - o, pairs)], pp_s.at[o], pp_r.at[o])
    total = jnp.sum(sum_p[...], axis=0)
    sum_s[side] = total
    send(sum_s.at[side], sum_s.at[side], ps_s, ps_r, sibling)
    arrived(sum_s.at[1 - side], ps_s, ps_r)
    mean_ref[0, 0] = jnp.sum(sum_s[0] + sum_s[1]) * scale
    sends.extend(half_copies())
    for i, dz in enumerate((1, 3, 2)):
        sends.extend(onward_rows(i, dz))
    for i, (dz, dy) in enumerate(STEPS):
        sends.extend([columns_copy(i, dz, dy), onward_columns(i, dz, dy)])
    sends.append(own_columns())
    for copy in sends:
        copy.wait_send()
    for i in range(4):
        out_copy(i, pl.ds(i * 256, 256)).wait()


def body(face_out, face_in, face_shared):
    dma = pltpu.SemaphoreType.DMA
    vmem = pltpu.VMEM
    sems = [dma, dma, dma((3,)), dma((3,)), dma((4, 3)), dma((4, 3)), dma((16,)), dma((16,)), dma((2,)), dma((2,)), dma((2,)),
            dma((2,)), dma((4, 3)), dma((4, 3)), dma((15,)), dma((15,)), dma((16,)), dma((16,)), dma((15,)), dma((15,)),
            dma((16,)), dma((16,)), dma, dma, dma((4,))]
    entries = 16 * 2 * 3840 * 2048
    out, mean = pl.pallas_call(
        lambda *refs: kernel(1.0 / entries, *refs),
        out_shape=(jax.ShapeDtypeStruct((1, 2, 240, 1024), F32), jax.ShapeDtypeStruct((1, 1), F32)),
        in_specs=[pl.BlockSpec(memory_space=vmem)] * 3,
        out_specs=(pl.BlockSpec(memory_space=pl.ANY), pl.BlockSpec(memory_space=pltpu.SMEM)),
        scratch_shapes=[vmem((768, 768), F32), vmem((768, 768), F32), vmem((1024, 768), F32), vmem((16, 48, 256), F32),
                        vmem((2, 768, 256), F32), vmem((2, 256, 768), BF16), vmem((2, 256, 768), BF16), vmem((24, 768), F32),
                        vmem((2, 240, 1024), F32), vmem((G, NB), F32),
                        vmem((8, 128), F32), vmem((16, 8, 128), F32), vmem((16, 8, 128), F32), vmem((2, 8, 128), F32)] + sems,
        compiler_params=pltpu.CompilerParams(collective_id=0, has_side_effects=True, vmem_limit_bytes=56 << 20),
        name="merge",
    )(face_out, face_in, face_shared)
    return out, mean[0, 0]


def solution(mesh):
    in_specs = (P("pair", ("side", "rows"), None), P("pair", "rows", "side"), P("pair", "side", "rows", None))
    out_specs = (P("pair", None, "rows", "side"), P())
    return jax.shard_map(body, mesh=mesh, in_specs=in_specs, out_specs=out_specs, check_vma=False)
```

```python
import jax
import jax.numpy as jnp
from jax import lax
from jax.experimental import pallas as pl
from jax.experimental.pallas import tpu as pltpu
from jax.sharding import PartitionSpec as P

MESH = pl.DeviceIdType.MESH
F32 = jnp.float32
BF16 = jnp.bfloat16
NB = 128
R = 32
G = 8
Y = 4
ZH = 4
Z = 16
ROWS = Y * ZH
STEPS = ((0, 1), (0, 3), (0, 2), (1, 0), (3, 0), (1, 1), (1, 3), (3, 1), (3, 3), (1, 2), (3, 2), (2, 0), (2, 1), (2, 3), (2, 2))


def sweep_tile(tile, one):
    row = lax.broadcasted_iota(jnp.int32, (G, NB), 0)
    lane = lax.broadcasted_iota(jnp.int32, (G, NB), 1)
    prow = lax.broadcasted_iota(jnp.int32, (R, NB), 0)
    plane = lax.broadcasted_iota(jnp.int32, (R, NB), 1)
    wide = lax.broadcasted_iota(jnp.int32, (NB, NB), 1)
    for p in range(0, NB, R):
        rows = tile[p : p + R, :]
        before = jnp.where((plane >= p) & (plane < p + R), jnp.where(plane - p == prow, -1.0, 0.0), rows)
        for g in range(0, R, G):
            k = p + g
            cols = [jnp.broadcast_to(rows[:, k + u : k + u + 1], (R, NB)) for u in range(G)]
            pivots = rows[g : g + G, :]
            inside = (lane >= k) & (lane < k + G)
            marked = jnp.where(inside, jnp.where(lane - k == row, -1.0, 0.0), pivots)
            v = [jnp.broadcast_to(marked[t : t + 1, :], (G, NB)) for t in range(G)]
            d = {}
            for t in range(G):
                full = jnp.broadcast_to(pivots[t : t + 1, :], (G, NB)) * one
                for u in range(t, G):
                    d[t, u] = jnp.broadcast_to(full[:, k + u : k + u + 1], (G, NB))
            r, low = [None] * G, {}
            for t in range(G):
                r[t] = 1.0 / d[t, t]
                for u in range(t + 1, G):
                    low[t, u] = d[t, u] * r[t]
                for u in range(t + 1, G):
                    for x in range(u, G):
                        d[u, x] = d[u, x] - low[t, u] * d[t, x]
                    v[u] = v[u] - low[t, u] * v[t]
            w = [v[t] * r[t] for t in range(G)]
            for t in range(G - 1, 0, -1):
                for u in range(t):
                    w[u] = w[u] - low[u, t] * w[t]
            packed = w[0]
            for t in range(1, G):
                packed = jnp.where(row == t, w[t], packed)
            acc = jnp.where((plane >= k) & (plane < k + G), 0.0, rows)
            for t in range(G):
                acc = acc - cols[t] * jnp.broadcast_to(w[t][0:1, :], (R, NB))
            rows = jnp.concatenate([x for x in (acc[:g], packed, acc[g + G :]) if x.shape[0]], axis=0)
        rest = jnp.where((wide >= p) & (wide < p + R), 0.0, tile)
        rest = rest - lax.dot_general(
            before, rows, (((0,), (0,)), ((), ())), precision=lax.Precision.HIGHEST, preferred_element_type=F32
        )
        tile = jnp.concatenate([x for x in (rest[:p], rows, rest[p + R :]) if x.shape[0]], axis=0)
    return tile


def split(x):
    hi = x.astype(BF16)
    return hi, (x - hi.astype(F32)).astype(BF16)


def dot3(a, b, dims):
    (ah, al), (bh, bl) = a, b
    one = lambda x, y: lax.dot_general(x, y, (dims, ((), ())), preferred_element_type=F32)
    return one(ah, bh) + (one(ah, bl) + one(al, bh))


def kernel(scale, panel_ref, in_ref, shared_ref, out_ref, mean_ref, schur, inv, rows_a, pieces, cols_b, xt_hi, xt_lo,
           half_in, one, acc, sum_z, sum_xy, half_s, half_r, sz_s, sz_r, sy_s, sy_r, sx_s, sx_r, az_s, az_r, ah_s, ah_r, ay_s, ay_r,
           b_s, b_r, bx_s, bx_r, ay4_s, ay4_r, pz_s, pz_r, pxy_s, pxy_r):
    me = lax.axis_index("rows")
    side = lax.axis_index("side")
    pair = lax.axis_index("pair")
    zh, y = me // Y, lax.rem(me, Y)
    n = 768
    half = 24
    width = 240
    z, x = zh * Y + lax.rem(pair, Y), pair // Y

    def at(dz, dy):
        return lax.rem(zh + dz, ZH) * Y + lax.rem(y + dy, Y)

    def back(dz, dy):
        return lax.rem(zh + ZH - dz, ZH) * Y + lax.rem(y + Y - dy, Y)

    def on_line(o):
        there = lax.rem(z + o, Z)
        return {"rows": there // ZH * Y + y, "pair": x * Y + lax.rem(there, ZH)}

    def on_plane(dx, dy, other):
        there = {"rows": at(0, dy), "pair": lax.rem(x + dx, Y) * Y + lax.rem(pair, Y)}
        return there | ({"side": 1 - side} if other else {})

    sibling = {"side": 1 - side}

    def remote(src, dst, send, recv, device):
        return pltpu.make_async_remote_copy(
            src_ref=src, dst_ref=dst, send_sem=send, recv_sem=recv, device_id=device, device_id_type=MESH
        )

    sends = []

    def send(src, dst, s, r, device):
        copy = remote(src, dst, s, r, device)
        copy.start()
        sends.append(copy)

    def arrived(dst, s, r):
        remote(dst, dst, s, r, sibling).wait_recv()

    barrier = pltpu.get_barrier_semaphore()
    pl.semaphore_signal(barrier, inc=1, device_id=sibling, device_id_type=MESH)
    for dz, dy in STEPS:
        pl.semaphore_signal(barrier, inc=1, device_id={"rows": at(dz, dy)}, device_id_type=MESH)
    line = [on_line(o) for o in range(1, Z) if o % ZH]
    plane = [on_plane(dx, dy, False) for dx, dy in STEPS if dx] + [on_plane(dx, dy, True) for dx, dy in STEPS]
    for device in line + plane:
        pl.semaphore_signal(barrier, inc=1, device_id=device, device_id_type=MESH)

    def strip(ref, r, s):
        return ref.at[pl.ds(pl.multiple_of((r * 2 + s) * half, 8), half), :]

    def panel_at(r):
        return rows_a.at[pl.ds(pl.multiple_of(r * 64, 64), 64), :]

    def quarter_at(r, q):
        return rows_a.at[pl.ds(pl.multiple_of(r * 64 + q * 16, 16), 16), :]

    def columns_at(s, r):
        return cols_b.at[s, pl.ds(pl.multiple_of(r * 48, 16), 48), :]

    for r in range(ROWS):
        pieces[r, :, 0:width] = in_ref[0, :, r * width : (r + 1) * width]
        pieces[r, :, width:256] = jnp.zeros((48, 256 - width), F32)
    panel_at(me)[...] = panel_ref[0]
    columns_at(side, me)[...] = pieces[me]
    one[...] = jnp.ones((G, NB), F32)
    pl.semaphore_wait(barrier, ROWS + len(line) + len(plane))

    def columns_copy(i, dz, dy):
        return remote(pieces.at[at(dz, dy)], columns_at(side, me), b_s.at[i], b_r.at[i], {"rows": at(dz, dy)})

    for i in (3, 4):
        columns_copy(i, *STEPS[i]).start()

    theirs = shared_ref.at[0, 0, pl.ds(pl.multiple_of((1 - side) * half, 8), half), :]
    send(theirs, half_in, half_s, half_r, sibling)
    arrived(half_in, half_s, half_r)
    mine = strip(schur, me, side)
    mine[...] = shared_ref[0, 0, pl.ds(pl.multiple_of(side * half, 8), half), :] + half_in[...]
    for i, dz in enumerate((1, 3, 2)):
        send(mine, mine, sz_s.at[i], sz_r.at[i], {"rows": at(dz, 0)})
    for i, dy in enumerate((1, 3, 2)):
        send(mine, mine, sy_s.at[0, i], sy_r.at[0, i], {"rows": at(0, dy)})
    send(mine, mine, sx_s.at[0], sx_r.at[0], sibling)

    panel = panel_ref.at[0]
    for i, dz in enumerate((1, 3)):
        send(panel, panel_at(me), az_s.at[i], az_r.at[i], {"rows": at(dz, 0)})

    for i, dz in enumerate((1, 3, 2)):
        got = strip(schur, back(dz, 0), side)
        arrived(got, sz_s.at[i], sz_r.at[i])
        for j, dy in enumerate((1, 3, 2)):
            send(got, got, sy_s.at[i + 1, j], sy_r.at[i + 1, j], {"rows": at(0, dy)})
        send(got, got, sx_s.at[i + 1], sx_r.at[i + 1], sibling)

    for i in (0, 1, 2, *range(5, 15)):
        columns_copy(i, *STEPS[i]).start()
    for j, dy in enumerate((1, 3, 2)):
        send(panel, panel_at(me), ay_s.at[0, j], ay_r.at[0, j], {"rows": at(0, dy)})
    for i, dz in enumerate((0, 1, 3, 2)):
        for j, dy in enumerate((1, 3, 2)):
            got = strip(schur, back(dz, dy), side)
            arrived(got, sy_s.at[i, j], sy_r.at[i, j])
            send(got, got, sx_s.at[4 + i * 3 + j], sx_r.at[4 + i * 3 + j], sibling)
    for i, dz in enumerate((0, 1, 3, 2)):
        arrived(strip(schur, back(dz, 0), 1 - side), sx_s.at[i], sx_r.at[i])
    for i, dz in enumerate((0, 1, 3, 2)):
        for j, dy in enumerate((1, 3, 2)):
            arrived(strip(schur, back(dz, dy), 1 - side), sx_s.at[4 + i * 3 + j], sx_r.at[4 + i * 3 + j])

    def onward_rows(i, dz):
        got = panel_at(back(dz, 0))
        return [
            remote(got, got, ay_s.at[i + 1, j], ay_r.at[i + 1, j], {"rows": at(0, dy)}) for j, dy in enumerate((1, 3, 2))
        ]

    def start_rows(i, dz):
        for copy in onward_rows(i, dz):
            copy.start()

    def half_copies():
        return [
            remote(
                quarter_at(back(dz, 0), q), quarter_at(back(dz, 0), q), ah_s.at[q], ah_r.at[q], {"rows": at(dz, 0)}
            )
            for dz, q in ((1, 0), (3, 3), (1, 1), (3, 2))
        ]

    def onward_quarter(q):
        got = quarter_at(back(2, 0), q)
        return [remote(got, got, ay4_s.at[q, j], ay4_r.at[q, j], {"rows": at(0, dy)}) for j, dy in enumerate((1, 3, 2))]

    def relay_quarter(q):
        arrived(quarter_at(back(2, 0), q), ah_s.at[q], ah_r.at[q])
        for copy in onward_quarter(q):
            copy.start()

    def onward_columns(i, dz, dy):
        got = columns_at(side, back(dz, dy))
        return remote(got, got, bx_s.at[i], bx_r.at[i], sibling)

    def own_columns():
        got = columns_at(side, me)
        return remote(got, got, bx_s.at[15], bx_r.at[15], sibling)

    def relay_columns(i, dz, dy):
        arrived(columns_at(side, back(dz, dy)), b_s.at[i], b_r.at[i])
        onward_columns(i, dz, dy).start()

    inv[...] = schur[...]

    @pl.loop(0, n // NB)
    def _(b):
        @pl.when(b == 1)
        def _():
            for i, dz in enumerate((1, 3)):
                arrived(panel_at(back(dz, 0)), az_s.at[i], az_r.at[i])
            for copy in half_copies():
                copy.start()
            start_rows(0, 1)
            start_rows(1, 3)

        @pl.when(b == 5)
        def _():
            own_columns().start()
            for i in range(11):
                relay_columns(i, *STEPS[i])

        block = pl.ds(pl.multiple_of(b * NB, NB), NB)
        swept = sweep_tile(inv[block, block], one[...])
        eye = lax.broadcasted_iota(jnp.int32, (NB, NB), 0) == lax.broadcasted_iota(jnp.int32, (NB, NB), 1)
        column = inv[:, block]
        inv[block, block] = jnp.where(eye, -1.0, 0.0)
        w = jnp.dot(swept, inv[block, :], precision=lax.Precision.HIGHEST, preferred_element_type=F32)
        inv[:, block] = jnp.zeros((n, NB), F32)
        inv[...] = inv[...] + jnp.dot(column, w, precision=lax.Precision.HIGHEST, preferred_element_type=F32)
        inv[block, :] = -w

    inverse = split(inv[...])
    for i in range(11, 15):
        relay_columns(i, *STEPS[i])

    def solve(b):
        xt_hi[b], xt_lo[b] = split(dot3(split(cols_b[b].T), inverse, ((1,), (0,))))

    solve(side)
    for q in (0, 3):
        relay_quarter(q)
    arrived(columns_at(1 - side, me), bx_s.at[15], bx_r.at[15])
    for i, (dz, dy) in enumerate(STEPS):
        arrived(columns_at(1 - side, back(dz, dy)), bx_s.at[i], bx_r.at[i])
    solve(1 - side)
    for q in (1, 2):
        relay_quarter(q)
    for i, dz in enumerate((0, 1, 3)):
        for j, dy in enumerate((1, 3, 2)):
            arrived(panel_at(back(dz, dy)), ay_s.at[i, j], ay_r.at[i, j])

    acc[...] = jnp.zeros((8, 128), F32)

    def tile_of(i):
        return pl.ds(pl.multiple_of(lax.rem(zh + i + i // 2 - i // 3 * 2, ZH) * 256, 256), 256)

    def out_copy(i):
        return pltpu.make_async_copy(product.at[:, :, tile_of(i)], out_ref.at[0, :, :, tile_of(i)], o_s.at[i])

    @pl.loop(0, ZH)
    def _(i):
        @pl.when(i == ZH - 1)
        def _():
            for q in (0, 3, 1, 2):
                for j, dy in enumerate((1, 3, 2)):
                    arrived(quarter_at(back(2, dy), q), ay4_s.at[q, j], ay4_r.at[q, j])

        tile = tile_of(i)
        a = split(rows_a[tile, :])
        for b in range(2):
            c = dot3((xt_hi[b], xt_lo[b]), a, ((1,), (1,)))[:width]
            out_ref[0, b, :, tile] = c
            s = jnp.sum((c * c).reshape(width // 8, 8, 256), axis=0)
            acc[...] = acc[...] + (s[:, :128] + s[:, 128:])

    sum_z[z] = acc[...]
    for o in range(1, Z):
        send(acc, sum_z.at[z], pz_s.at[o], pz_r.at[o], on_line(o))
    for o in range(1, Z):
        arrived(sum_z.at[lax.rem(z + Z - o, Z)], pz_s.at[o], pz_r.at[o])
    mine = sum_xy.at[side, x * Y + y]
    mine[...] = jnp.sum(sum_z[...], axis=0)
    for other in range(2):
        for i, (dx, dy) in enumerate(((0, 0), *STEPS)[1 - other :]):
            send(mine, mine, pxy_s.at[other, i], pxy_r.at[other, i], on_plane(dx, dy, other))
    for other in range(2):
        for i, (dx, dy) in enumerate(((0, 0), *STEPS)[1 - other :]):
            slot = lax.rem(x + Y - dx, Y) * Y + lax.rem(y + Y - dy, Y)
            arrived(sum_xy.at[1 - side if other else side, slot], pxy_s.at[other, i], pxy_r.at[other, i])
    mean_ref[0, 0] = jnp.sum(jnp.sum(sum_xy[...], axis=(0, 1))) * scale
    sends.extend(half_copies())
    for i, dz in enumerate((1, 3)):
        sends.extend(onward_rows(i, dz))
    for q in range(4):
        sends.extend(onward_quarter(q))
    for i, (dz, dy) in enumerate(STEPS):
        sends.extend([columns_copy(i, dz, dy), onward_columns(i, dz, dy)])
    sends.append(own_columns())
    for copy in sends:
        copy.wait_send()


def body(face_out, face_in, face_shared):
    dma = pltpu.SemaphoreType.DMA
    vmem = pltpu.VMEM
    shapes = ((), (3,), (4, 3), (16,), (2,), (4,), (3, 3), (15,), (16,), (4, 3), (Z,), (2, 16))
    sems = [dma(s) if s else dma for s in shapes for _ in range(2)]
    entries = 16 * 2 * 3840 * 2048
    out, mean = pl.pallas_call(
        lambda *refs: kernel(1.0 / entries, *refs),
        out_shape=(vmem((1, 2, 240, 1024), F32), jax.ShapeDtypeStruct((1, 1), F32)),
        in_specs=[pl.BlockSpec(memory_space=vmem)] * 3,
        out_specs=(pl.BlockSpec(memory_space=vmem), pl.BlockSpec(memory_space=pltpu.SMEM)),
        scratch_shapes=[vmem((768, 768), F32), vmem((768, 768), F32), vmem((1024, 768), F32), vmem((16, 48, 256), F32),
                        vmem((2, 768, 256), F32), vmem((2, 256, 768), BF16), vmem((2, 256, 768), BF16), vmem((24, 768), F32),
                        vmem((G, NB), F32),
                        vmem((8, 128), F32), vmem((Z, 8, 128), F32), vmem((2, 16, 8, 128), F32)] + sems,
        compiler_params=pltpu.CompilerParams(collective_id=0, has_side_effects=True, vmem_limit_bytes=56 << 20),
        name="merge",
    )(face_out, face_in, face_shared)
    return out, mean[0, 0]


def solution(mesh):
    in_specs = (P("pair", ("side", "rows"), None), P("pair", "rows", "side"), P("pair", "side", "rows", None))
    out_specs = (P("pair", None, "rows", "side"), P())
    return jax.shard_map(body, mesh=mesh, in_specs=in_specs, out_specs=out_specs, check_vma=False)
```

```python
import jax
import jax.numpy as jnp
from jax import lax
from jax.experimental import pallas as pl
from jax.experimental.pallas import tpu as pltpu
from jax.sharding import PartitionSpec as P

MESH = pl.DeviceIdType.MESH
F32 = jnp.float32
BF16 = jnp.bfloat16
NB = 128
R = 32
G = 8
Y = 4
ZH = 4
ROWS = Y * ZH
STEPS = ((0, 1), (0, 3), (0, 2), (1, 0), (3, 0), (1, 1), (1, 3), (3, 1), (3, 3), (1, 2), (3, 2), (2, 0), (2, 1), (2, 3), (2, 2))


def sweep_tile(tile, one):
    row = lax.broadcasted_iota(jnp.int32, (G, NB), 0)
    lane = lax.broadcasted_iota(jnp.int32, (G, NB), 1)
    prow = lax.broadcasted_iota(jnp.int32, (R, NB), 0)
    plane = lax.broadcasted_iota(jnp.int32, (R, NB), 1)
    wide = lax.broadcasted_iota(jnp.int32, (NB, NB), 1)
    for p in range(0, NB, R):
        rows = tile[p : p + R, :]
        before = jnp.where((plane >= p) & (plane < p + R), jnp.where(plane - p == prow, -1.0, 0.0), rows)
        for g in range(0, R, G):
            k = p + g
            cols = [jnp.broadcast_to(rows[:, k + u : k + u + 1], (R, NB)) for u in range(G)]
            pivots = rows[g : g + G, :]
            inside = (lane >= k) & (lane < k + G)
            marked = jnp.where(inside, jnp.where(lane - k == row, -1.0, 0.0), pivots)
            v = [jnp.broadcast_to(marked[t : t + 1, :], (G, NB)) for t in range(G)]
            d = {}
            for t in range(G):
                full = jnp.broadcast_to(pivots[t : t + 1, :], (G, NB)) * one
                for u in range(t, G):
                    d[t, u] = jnp.broadcast_to(full[:, k + u : k + u + 1], (G, NB))
            r, low = [None] * G, {}
            for t in range(G):
                r[t] = 1.0 / d[t, t]
                for u in range(t + 1, G):
                    low[t, u] = d[t, u] * r[t]
                for u in range(t + 1, G):
                    for x in range(u, G):
                        d[u, x] = d[u, x] - low[t, u] * d[t, x]
                    v[u] = v[u] - low[t, u] * v[t]
            w = [v[t] * r[t] for t in range(G)]
            for t in range(G - 1, 0, -1):
                for u in range(t):
                    w[u] = w[u] - low[u, t] * w[t]
            packed = w[0]
            for t in range(1, G):
                packed = jnp.where(row == t, w[t], packed)
            acc = jnp.where((plane >= k) & (plane < k + G), 0.0, rows)
            for t in range(G):
                acc = acc - cols[t] * jnp.broadcast_to(w[t][0:1, :], (R, NB))
            rows = jnp.concatenate([x for x in (acc[:g], packed, acc[g + G :]) if x.shape[0]], axis=0)
        rest = jnp.where((wide >= p) & (wide < p + R), 0.0, tile)
        rest = rest - lax.dot_general(
            before, rows, (((0,), (0,)), ((), ())), precision=lax.Precision.HIGHEST, preferred_element_type=F32
        )
        tile = jnp.concatenate([x for x in (rest[:p], rows, rest[p + R :]) if x.shape[0]], axis=0)
    return tile


def split(x):
    hi = x.astype(BF16)
    return hi, (x - hi.astype(F32)).astype(BF16)


def dot3(a, b, dims):
    (ah, al), (bh, bl) = a, b
    one = lambda x, y: lax.dot_general(x, y, (dims, ((), ())), preferred_element_type=F32)
    return one(ah, bh) + (one(ah, bl) + one(al, bh))


def kernel(scale, panel_ref, in_ref, shared_ref, out_ref, mean_ref, schur, inv, rows_a, pieces, cols_b, xt_hi, xt_lo,
           half_in, one, acc, sum_r, sum_p, sum_s, half_s, half_r, sz_s, sz_r, sy_s, sy_r, sx_s, sx_r, az_s, az_r, ah_s, ah_r, ay_s, ay_r,
           b_s, b_r, bx_s, bx_r, pr_s, pr_r, pp_s, pp_r, ps_s, ps_r):
    me = lax.axis_index("rows")
    side = lax.axis_index("side")
    pair = lax.axis_index("pair")
    zh, y = me // Y, lax.rem(me, Y)
    n = 768
    half = 24
    width = 240
    pairs = 16

    def at(dz, dy):
        return lax.rem(zh + dz, ZH) * Y + lax.rem(y + dy, Y)

    def back(dz, dy):
        return lax.rem(zh + ZH - dz, ZH) * Y + lax.rem(y + Y - dy, Y)

    sibling = {"side": 1 - side}

    def remote(src, dst, send, recv, device):
        return pltpu.make_async_remote_copy(
            src_ref=src, dst_ref=dst, send_sem=send, recv_sem=recv, device_id=device, device_id_type=MESH
        )

    sends = []

    def send(src, dst, s, r, device):
        copy = remote(src, dst, s, r, device)
        copy.start()
        sends.append(copy)

    def arrived(dst, s, r):
        remote(dst, dst, s, r, sibling).wait_recv()

    barrier = pltpu.get_barrier_semaphore()
    pl.semaphore_signal(barrier, inc=1, device_id=sibling, device_id_type=MESH)
    for dz, dy in STEPS:
        pl.semaphore_signal(barrier, inc=1, device_id={"rows": at(dz, dy)}, device_id_type=MESH)
    for o in range(1, pairs):
        pl.semaphore_signal(barrier, inc=1, device_id={"pair": lax.rem(pair + o, pairs)}, device_id_type=MESH)

    def strip(ref, r, s):
        return ref.at[pl.ds(pl.multiple_of((r * 2 + s) * half, 8), half), :]

    def panel_at(r):
        return rows_a.at[pl.ds(pl.multiple_of(r * 64, 64), 64), :]

    def half_panel_at(r, h):
        return rows_a.at[pl.ds(pl.multiple_of(r * 64 + h * 32, 32), 32), :]

    def columns_at(s, r):
        return cols_b.at[s, pl.ds(pl.multiple_of(r * 48, 16), 48), :]

    for r in range(ROWS):
        pieces[r, :, 0:width] = in_ref[0, :, r * width : (r + 1) * width]
        pieces[r, :, width:256] = jnp.zeros((48, 256 - width), F32)
    panel_at(me)[...] = panel_ref[0]
    columns_at(side, me)[...] = pieces[me]
    one[...] = jnp.ones((G, NB), F32)
    pl.semaphore_wait(barrier, ROWS + pairs - 1)

    theirs = shared_ref.at[0, 0, pl.ds(pl.multiple_of((1 - side) * half, 8), half), :]
    send(theirs, half_in, half_s, half_r, sibling)
    arrived(half_in, half_s, half_r)
    mine = strip(schur, me, side)
    mine[...] = shared_ref[0, 0, pl.ds(pl.multiple_of(side * half, 8), half), :] + half_in[...]
    for i, dz in enumerate((1, 3, 2)):
        send(mine, mine, sz_s.at[i], sz_r.at[i], {"rows": at(dz, 0)})
    for i, dy in enumerate((1, 3, 2)):
        send(mine, mine, sy_s.at[0, i], sy_r.at[0, i], {"rows": at(0, dy)})
    send(mine, mine, sx_s.at[0], sx_r.at[0], sibling)

    panel = panel_ref.at[0]
    for i, dz in enumerate((1, 3)):
        send(panel, panel_at(me), az_s.at[i], az_r.at[i], {"rows": at(dz, 0)})

    for i, dz in enumerate((1, 3, 2)):
        got = strip(schur, back(dz, 0), side)
        arrived(got, sz_s.at[i], sz_r.at[i])
        for j, dy in enumerate((1, 3, 2)):
            send(got, got, sy_s.at[i + 1, j], sy_r.at[i + 1, j], {"rows": at(0, dy)})
        send(got, got, sx_s.at[i + 1], sx_r.at[i + 1], sibling)

    def columns_copy(i, dz, dy):
        return remote(pieces.at[at(dz, dy)], columns_at(side, me), b_s.at[i], b_r.at[i], {"rows": at(dz, dy)})

    for i in range(11):
        columns_copy(i, *STEPS[i]).start()
    for j, dy in enumerate((1, 3, 2)):
        send(panel, panel_at(me), ay_s.at[0, j], ay_r.at[0, j], {"rows": at(0, dy)})
    for i, dz in enumerate((0, 1, 3, 2)):
        for j, dy in enumerate((1, 3, 2)):
            got = strip(schur, back(dz, dy), side)
            arrived(got, sy_s.at[i, j], sy_r.at[i, j])
            send(got, got, sx_s.at[4 + i * 3 + j], sx_r.at[4 + i * 3 + j], sibling)
    for i, dz in enumerate((0, 1, 3, 2)):
        arrived(strip(schur, back(dz, 0), 1 - side), sx_s.at[i], sx_r.at[i])
    for i, dz in enumerate((0, 1, 3, 2)):
        for j, dy in enumerate((1, 3, 2)):
            arrived(strip(schur, back(dz, dy), 1 - side), sx_s.at[4 + i * 3 + j], sx_r.at[4 + i * 3 + j])

    def onward_rows(i, dz):
        got = panel_at(back(dz, 0))
        return [
            remote(got, got, ay_s.at[i + 1, j], ay_r.at[i + 1, j], {"rows": at(0, dy)}) for j, dy in enumerate((1, 3, 2))
        ]

    def start_rows(i, dz):
        for copy in onward_rows(i, dz):
            copy.start()

    def half_copies():
        first, last = half_panel_at(back(1, 0), 0), half_panel_at(back(3, 0), 1)
        return [
            remote(first, first, ah_s.at[0], ah_r.at[0], {"rows": at(1, 0)}),
            remote(last, last, ah_s.at[1], ah_r.at[1], {"rows": at(3, 0)}),
        ]

    def onward_columns(i, dz, dy):
        got = columns_at(side, back(dz, dy))
        return remote(got, got, bx_s.at[i], bx_r.at[i], sibling)

    def own_columns():
        got = columns_at(side, me)
        return remote(got, got, bx_s.at[15], bx_r.at[15], sibling)

    def relay_columns(i, dz, dy):
        arrived(columns_at(side, back(dz, dy)), b_s.at[i], b_r.at[i])
        onward_columns(i, dz, dy).start()

    inv[...] = schur[...]

    @pl.loop(0, n // NB)
    def _(b):
        @pl.when(b == 1)
        def _():
            for i, dz in enumerate((1, 3)):
                arrived(panel_at(back(dz, 0)), az_s.at[i], az_r.at[i])
            for copy in half_copies():
                copy.start()
            for i in range(11, 15):
                columns_copy(i, *STEPS[i]).start()
            start_rows(0, 1)
            start_rows(1, 3)

        @pl.when(b == 4)
        def _():
            own_columns().start()
            for i in range(11):
                relay_columns(i, *STEPS[i])

        @pl.when(b == 5)
        def _():
            for h in range(2):
                arrived(half_panel_at(back(2, 0), h), ah_s.at[h], ah_r.at[h])
            start_rows(2, 2)

        block = pl.ds(pl.multiple_of(b * NB, NB), NB)
        swept = sweep_tile(inv[block, block], one[...])
        eye = lax.broadcasted_iota(jnp.int32, (NB, NB), 0) == lax.broadcasted_iota(jnp.int32, (NB, NB), 1)
        column = inv[:, block]
        inv[block, block] = jnp.where(eye, -1.0, 0.0)
        w = jnp.dot(swept, inv[block, :], precision=lax.Precision.HIGHEST, preferred_element_type=F32)
        inv[:, block] = jnp.zeros((n, NB), F32)
        inv[...] = inv[...] + jnp.dot(column, w, precision=lax.Precision.HIGHEST, preferred_element_type=F32)
        inv[block, :] = -w

    inverse = split(inv[...])
    for i in range(11, 15):
        relay_columns(i, *STEPS[i])

    def solve(b):
        xt_hi[b], xt_lo[b] = split(dot3(split(cols_b[b].T), inverse, ((1,), (0,))))

    solve(side)
    arrived(columns_at(1 - side, me), bx_s.at[15], bx_r.at[15])
    for i, (dz, dy) in enumerate(STEPS):
        arrived(columns_at(1 - side, back(dz, dy)), bx_s.at[i], bx_r.at[i])
    solve(1 - side)
    for i, dz in enumerate((0, 1, 3, 2)):
        for j, dy in enumerate((1, 3, 2)):
            arrived(panel_at(back(dz, dy)), ay_s.at[i, j], ay_r.at[i, j])

    acc[...] = jnp.zeros((8, 128), F32)

    def out_copy(i, tile):
        return pltpu.make_async_copy(product.at[:, :, tile], out_ref.at[0, :, :, tile], o_s.at[i])

    @pl.loop(0, 4)
    def _(i):
        tile = pl.ds(pl.multiple_of(i * 256, 256), 256)
        a = split(rows_a[tile, :])
        for b in range(2):
            c = dot3((xt_hi[b], xt_lo[b]), a, ((1,), (1,)))[:width]
            out_ref[0, b, :, tile] = c
            s = jnp.sum((c * c).reshape(width // 8, 8, 256), axis=0)
            acc[...] = acc[...] + (s[:, :128] + s[:, 128:])

    sum_r[me] = acc[...]
    for i, (dz, dy) in enumerate(STEPS):
        send(acc, sum_r.at[me], pr_s.at[i], pr_r.at[i], {"rows": at(dz, dy)})
    for i, (dz, dy) in enumerate(STEPS):
        arrived(sum_r.at[back(dz, dy)], pr_s.at[i], pr_r.at[i])
    sum_p[pair] = jnp.sum(sum_r[...], axis=0)
    for o in range(1, pairs):
        send(sum_p.at[pair], sum_p.at[pair], pp_s.at[o], pp_r.at[o], {"pair": lax.rem(pair + o, pairs)})
    for o in range(1, pairs):
        arrived(sum_p.at[lax.rem(pair + pairs - o, pairs)], pp_s.at[o], pp_r.at[o])
    total = jnp.sum(sum_p[...], axis=0)
    sum_s[side] = total
    send(sum_s.at[side], sum_s.at[side], ps_s, ps_r, sibling)
    arrived(sum_s.at[1 - side], ps_s, ps_r)
    mean_ref[0, 0] = jnp.sum(sum_s[0] + sum_s[1]) * scale
    sends.extend(half_copies())
    for i, dz in enumerate((1, 3, 2)):
        sends.extend(onward_rows(i, dz))
    for i, (dz, dy) in enumerate(STEPS):
        sends.extend([columns_copy(i, dz, dy), onward_columns(i, dz, dy)])
    sends.append(own_columns())
    for copy in sends:
        copy.wait_send()


def body(face_out, face_in, face_shared):
    dma = pltpu.SemaphoreType.DMA
    vmem = pltpu.VMEM
    sems = [dma, dma, dma((3,)), dma((3,)), dma((4, 3)), dma((4, 3)), dma((16,)), dma((16,)), dma((2,)), dma((2,)), dma((2,)),
            dma((2,)), dma((4, 3)), dma((4, 3)), dma((15,)), dma((15,)), dma((16,)), dma((16,)), dma((15,)), dma((15,)),
            dma((16,)), dma((16,)), dma, dma]
    entries = 16 * 2 * 3840 * 2048
    out, mean = pl.pallas_call(
        lambda *refs: kernel(1.0 / entries, *refs),
        out_shape=(vmem((1, 2, 240, 1024), F32), jax.ShapeDtypeStruct((1, 1), F32)),
        in_specs=[pl.BlockSpec(memory_space=vmem)] * 3,
        out_specs=(pl.BlockSpec(memory_space=vmem), pl.BlockSpec(memory_space=pltpu.SMEM)),
        scratch_shapes=[vmem((768, 768), F32), vmem((768, 768), F32), vmem((1024, 768), F32), vmem((16, 48, 256), F32),
                        vmem((2, 768, 256), F32), vmem((2, 256, 768), BF16), vmem((2, 256, 768), BF16), vmem((24, 768), F32),
                        vmem((G, NB), F32),
                        vmem((8, 128), F32), vmem((16, 8, 128), F32), vmem((16, 8, 128), F32), vmem((2, 8, 128), F32)] + sems,
        compiler_params=pltpu.CompilerParams(collective_id=0, has_side_effects=True, vmem_limit_bytes=56 << 20),
        name="merge",
    )(face_out, face_in, face_shared)
    return out, mean[0, 0]


def solution(mesh):
    in_specs = (P("pair", ("side", "rows"), None), P("pair", "rows", "side"), P("pair", "side", "rows", None))
    out_specs = (P("pair", None, "rows", "side"), P())
    return jax.shard_map(body, mesh=mesh, in_specs=in_specs, out_specs=out_specs, check_vma=False)
```
